32 devices in a mesh: gx: 8 (over y, x, core), gy: 4 (over z).
Axes of the slice: x: 2, y: 2, z: 4, core: 2. Of those that a mesh axis runs over, the one named last changes fastest.
Arguments:
- phase_pops: float32 [15, 16, 16, 512], P(None, 'gx', None, 'gy'), may hold values from 0 to 0.1
- flow_pops: float32 [19, 16, 16, 512], P(None, 'gx', None, 'gy'), may hold values from 0 to 0.1
- solid_flags: int32 [16, 16, 512], P('gx', None, 'gy'), may hold values 0 or 1
Outputs:
- phase_out: float32 [15, 16, 16, 512], P(None, 'gx', None, 'gy')
- flow_out: float32 [19, 16, 16, 512], P(None, 'gx', None, 'gy')
The draws below stay inside these ranges and needn't reach their ends.
All inputs are finite; a program needn't handle non-finite values. No bound on the sum of `solid_flags` on one device may be relied on, other than what follows from the above.
Results may differ from the reference program's by a relative error of at most 0.0001.
Values sent between devices are 32-bit elements; how exact they have to be, the bound alone decides.
A program may use at most 64 MiB of HBM per device.

```python
import jax
import jax.numpy as jnp
from jax import lax

STEPS = 2
NX = 16
NY = 512
NZ = 16


def set_ends(result, stream_key, smallest, largest):
    longest = result.shape.index(max(result.shape))
    spots = []
    for shift in (0, 1):
        where = [jax.random.randint(jax.random.fold_in(stream_key, axis), (), 0, length) for axis, length in enumerate(result.shape)]
        where[longest] = (where[longest] + shift) % result.shape[longest]
        spots.append(tuple(where))
    return result.at[spots[0]].set(smallest).at[spots[1]].set(largest)


def levels(rng, extent, pieces, low, top_value):
    def one(axis_at, blocks):
        draws = jax.random.uniform(jax.random.fold_in(jax.random.fold_in(rng, 6), axis_at), (blocks,), jnp.float32, low / len(pieces), top_value / len(pieces))
        return jnp.repeat(jnp.exp(draws), extent[axis_at] // blocks).reshape((-1,) + (1,) * (len(extent) - axis_at - 1))

    gain = one(*pieces[0])
    for cut in pieces[1:]:
        gain = gain * one(*cut)
    return gain


def setup_inputs(seed: int = 0) -> dict:
    arg_keys = jax.random.split(jax.random.key(seed), 4)
    return {
        "phase_pops": jnp.clip(0.1 * jax.random.uniform(arg_keys[0], (15, NX, NZ, NY), jnp.float32) ** levels(arg_keys[0], (15, NX, NZ, NY), ((1, 8), (3, 4)), -0.2, 0.2), 0.0, 0.1),
        "flow_pops": jnp.clip(0.1 * jax.random.uniform(arg_keys[1], (19, NX, NZ, NY), jnp.float32) ** levels(arg_keys[1], (19, NX, NZ, NY), ((1, 8), (3, 4)), -0.2, 0.2), 0.0, 0.1),
        "solid_flags": set_ends((jax.random.randint(arg_keys[2], (NX, NZ, NY), 0, 8) < 1).astype(jnp.int32), jax.random.fold_in(arg_keys[2], 1), 0, 1),
    }


PHASE_VELOCITIES = [(0, 0, 0), (1, 0, 0), (-1, 0, 0), (0, 1, 0), (0, -1, 0), (0, 0, 1), (0, 0, -1), (1, 1, 1), (1, 1, -1), (1, -1, 1), (1, -1, -1), (-1, 1, 1), (-1, 1, -1), (-1, -1, 1), (-1, -1, -1)]
PHASE_WEIGHTS = [2.0 / 9.0] + [1.0 / 9.0] * 6 + [1.0 / 72.0] * 8
FLOW_VELOCITIES = [(0, 0, 0), (1, 0, 0), (-1, 0, 0), (0, 1, 0), (0, -1, 0), (0, 0, 1), (0, 0, -1), (1, 1, 0), (1, -1, 0), (-1, 1, 0), (-1, -1, 0), (1, 0, 1), (1, 0, -1), (-1, 0, 1), (-1, 0, -1), (0, 1, 1), (0, 1, -1), (0, -1, 1), (0, -1, -1)]
FLOW_WEIGHTS = [1.0 / 3.0] + [1.0 / 18.0] * 6 + [1.0 / 36.0] * 12
SURFACE_TENSION = 0.05
INTERFACE_WIDTH = 4.0
GRADIENT_FLOOR = 0.1
PHASE_LAMBDA = 0.3
PHASE_RELAX = 0.8

def reverse_of(velocities):
    return [velocities.index((-vector[0], -vector[1], -vector[2])) for vector in velocities]

def relax(phase_read, flow_read, phase_field, neighbours, solid_cells):
    gradient = []
    for coordinate in range(3):
        total = jnp.zeros_like(phase_field)
        for number in range(19):
            if FLOW_VELOCITIES[number][coordinate] != 0:
                total = total + FLOW_WEIGHTS[number] * FLOW_VELOCITIES[number][coordinate] * neighbours[number]
        gradient.append(3.0 * total)
    laplacian = jnp.zeros_like(phase_field)
    for number in range(1, 19):
        laplacian = laplacian + FLOW_WEIGHTS[number] * (neighbours[number] - phase_field)
    laplacian = 6.0 * laplacian
    magnitude = jnp.sqrt(gradient[0] ** 2 + gradient[1] ** 2 + gradient[2] ** 2)
    scaling = 1.0 / jnp.maximum(magnitude, GRADIENT_FLOOR)
    normal = [component * scaling for component in gradient]
    clipped = jnp.clip(phase_field, 0.0, 1.0)
    density = 1.0 + 2.0 * clipped
    relax_time = 0.6 + 0.4 * clipped
    beta_value = 12.0 * SURFACE_TENSION / INTERFACE_WIDTH
    kappa_value = 1.5 * SURFACE_TENSION * INTERFACE_WIDTH
    potential = 4.0 * beta_value * phase_field * (phase_field - 1.0) * (phase_field - 0.5) - kappa_value * laplacian
    force_terms = [potential * component for component in gradient]
    pressure = lax.optimization_barrier(jnp.sum(flow_read, axis=0))
    velocity = []
    for coordinate in range(3):
        moment = 0.5 * force_terms[coordinate]
        for number in range(19):
            if FLOW_VELOCITIES[number][coordinate] != 0:
                moment = moment + FLOW_VELOCITIES[number][coordinate] * flow_read[number]
        velocity.append(moment / density)
    speed_sq = velocity[0] ** 2 + velocity[1] ** 2 + velocity[2] ** 2
    force_factor = 3.0 * (1.0 - 0.5 / relax_time) / density
    flow_reverse = reverse_of(FLOW_VELOCITIES)
    flow_post = []
    for number in range(19):
        vector = FLOW_VELOCITIES[number]
        weight = FLOW_WEIGHTS[number]
        along = vector[0] * velocity[0] + vector[1] * velocity[1] + vector[2] * velocity[2]
        along_force = vector[0] * force_terms[0] + vector[1] * force_terms[1] + vector[2] * force_terms[2]
        equilibrium = weight * (pressure + 3.0 * along + 4.5 * along * along - 1.5 * speed_sq)
        current = flow_read[number]
        post_value = current - (current - equilibrium) / relax_time + weight * force_factor * along_force
        flow_post.append(jnp.where(solid_cells, flow_read[flow_reverse[number]], post_value))
    phase_reverse = reverse_of(PHASE_VELOCITIES)
    interface = PHASE_LAMBDA * phase_field * (1.0 - phase_field)
    phase_post = []
    for number in range(15):
        vector = PHASE_VELOCITIES[number]
        weight = PHASE_WEIGHTS[number]
        along = vector[0] * velocity[0] + vector[1] * velocity[1] + vector[2] * velocity[2]
        along_normal = vector[0] * normal[0] + vector[1] * normal[1] + vector[2] * normal[2]
        equilibrium = weight * (phase_field * (1.0 + 3.0 * along) + interface * along_normal)
        current = phase_read[number]
        post_value = current - (current - equilibrium) / PHASE_RELAX
        phase_post.append(jnp.where(solid_cells, phase_read[phase_reverse[number]], post_value))
    return (jnp.stack(phase_post), jnp.stack(flow_post))

def roll_field(values, vector):
    return jnp.roll(values, (vector[0], vector[2], vector[1]), axis=(0, 1, 2))

def reference(phase_pops, flow_pops, solid_flags):
    solid_cells = solid_flags > 0
    for step in range(STEPS):
        phase_read = jnp.stack([roll_field(phase_pops[number], PHASE_VELOCITIES[number]) for number in range(15)])
        phase_field = lax.optimization_barrier(jnp.sum(phase_read, axis=0))
        flow_read = jnp.stack([roll_field(flow_pops[number], FLOW_VELOCITIES[number]) for number in range(19)])
        neighbours = [roll_field(phase_field, (-vector[0], -vector[1], -vector[2])) for vector in FLOW_VELOCITIES]
        phase_pops, flow_pops = relax(phase_read, flow_read, phase_field, neighbours, solid_cells)
    return (phase_pops, flow_pops)
```

```python
import functools

import jax
import jax.numpy as jnp
from jax import lax
from jax.experimental import pallas as pl
from jax.experimental.pallas import tpu as pltpu
from jax.sharding import PartitionSpec as P

STEPS = 2
PHASE_VELOCITIES = [
    (0, 0, 0), (1, 0, 0), (-1, 0, 0), (0, 1, 0), (0, -1, 0), (0, 0, 1), (0, 0, -1),
    (1, 1, 1), (1, 1, -1), (1, -1, 1), (1, -1, -1),
    (-1, 1, 1), (-1, 1, -1), (-1, -1, 1), (-1, -1, -1),
]
PHASE_WEIGHTS = [2.0 / 9.0] + [1.0 / 9.0] * 6 + [1.0 / 72.0] * 8
FLOW_VELOCITIES = [
    (0, 0, 0), (1, 0, 0), (-1, 0, 0), (0, 1, 0), (0, -1, 0), (0, 0, 1), (0, 0, -1),
    (1, 1, 0), (1, -1, 0), (-1, 1, 0), (-1, -1, 0),
    (1, 0, 1), (1, 0, -1), (-1, 0, 1), (-1, 0, -1),
    (0, 1, 1), (0, 1, -1), (0, -1, 1), (0, -1, -1),
]
FLOW_WEIGHTS = [1.0 / 3.0] + [1.0 / 18.0] * 6 + [1.0 / 36.0] * 12
SURFACE_TENSION = 0.05
INTERFACE_WIDTH = 4.0
GRADIENT_FLOOR = 0.1
PHASE_LAMBDA = 0.3
PHASE_RELAX = 0.8
BETA = 12.0 * SURFACE_TENSION / INTERFACE_WIDTH
KAPPA = 1.5 * SURFACE_TENSION * INTERFACE_WIDTH

MESH = pl.DeviceIdType.MESH
SIDES = [(-1, 0), (1, 0), (0, -1), (0, 1), (-1, -1), (-1, 1), (1, -1), (1, 1)]


def moving(velocities, coordinate, sign):
    return [n for n, vector in enumerate(velocities) if vector[coordinate] == sign]


CROSSING = {
    sign: [("h", n) for n in moving(PHASE_VELOCITIES, 0, sign)]
    + [("f", n) for n in moving(FLOW_VELOCITIES, 0, sign)]
    for sign in (1, -1)
}


def opposite(velocities, n):
    vector = velocities[n]
    return velocities.index((-vector[0], -vector[1], -vector[2]))


def slot_table(nx):
    slots = {}
    for sign in (1, -1):
        for kind, velocities in (("h", PHASE_VELOCITIES), ("f", FLOW_VELOCITIES)):
            for n in moving(velocities, 1, sign):
                for x in range(nx):
                    slots[kind, n, x] = len(slots)
    for kind in ("edge+", "edge-", "push+", "push-"):
        for x in range(-1, nx + 1):
            slots[kind, x] = len(slots)
    return slots


def kernel(
    size_gx, size_gy, phase_in, flow_in, solid_in, phase_out, flow_out,
    h_buf, f_buf, solid, slab_out, slab_in, pack_out, pack_in,
    load_sem, store_sem, slab_send, slab_recv, pack_send, pack_recv,
):
    nx, nz, ny = solid.shape
    slots = slot_table(nx)
    assert len(slots) <= ny
    gx, gy = lax.axis_index("gx"), lax.axis_index("gy")

    def device(side):
        return (lax.rem(gx + side[0] + size_gx, size_gx), lax.rem(gy + side[1] + size_gy, size_gy))

    loads = [
        pltpu.make_async_copy(phase_in, h_buf.at[0], load_sem.at[0]),
        pltpu.make_async_copy(flow_in, f_buf.at[0], load_sem.at[1]),
        pltpu.make_async_copy(solid_in, solid, load_sem.at[2]),
    ]
    for load in loads:
        load.start()
    barrier = pltpu.get_barrier_semaphore()
    for side in SIDES:
        pl.semaphore_signal(barrier, inc=1, device_id=device(side), device_id_type=MESH)

    lanes = lax.broadcasted_iota(jnp.int32, (nz, ny), 1)
    first, last = lanes == 0, lanes == ny - 1

    def turn(tile, shift, axis):
        shift %= tile.shape[axis]
        return pltpu.roll(tile, shift, axis) if shift else tile

    def up(tile):
        return turn(tile, -1, 0)

    def down(tile):
        return turn(tile, 1, 0)

    def pushes(step):
        grouped = {}
        for x in range(nx):
            for n, (cx, cy, cz) in enumerate(PHASE_VELOCITIES):
                value = turn(h_buf[step, n, x], cz, 0)
                key = (cy, x + cx)
                grouped[key] = grouped[key] + value if key in grouped else value
        inside = {}
        for x in range(-1, nx + 1):
            inside[x] = (
                grouped[0, x]
                + jnp.where(first, 0.0, turn(grouped[1, x], 1, 1))
                + jnp.where(last, 0.0, turn(grouped[-1, x], -1, 1))
            )
        packed = jnp.zeros((nz, ny), jnp.float32)
        for key, slot in slots.items():
            if key[0] in ("h", "f"):
                kind, n, x = key
                velocities, buf = (PHASE_VELOCITIES, h_buf) if kind == "h" else (FLOW_VELOCITIES, f_buf)
                sign, tile = velocities[n][1], buf[step, n, x]
            else:
                sign = 1 if key[0][-1] == "+" else -1
                tile = inside[key[1]] if key[0][:4] == "edge" else grouped[sign, key[1]]
            source = ny - 1 if sign == 1 else 0
            packed = jnp.where(lanes == slot, turn(tile, slot - source, 1), packed)
        pack_out[step, 0] = inside[0]
        pack_out[step, 1] = packed
        pack_out[step, 2] = inside[nx - 1]
        return grouped, inside, packed

    def fill_slab(step):
        for place, sign in enumerate((-1, 1)):
            x = 0 if sign == -1 else nx - 1
            for k, (kind, n) in enumerate(CROSSING[sign]):
                slab_out[step, place, k] = (h_buf if kind == "h" else f_buf)[step, n, x]

    def slab_copies(step):
        return [
            pltpu.make_async_remote_copy(
                slab_out.at[step, place], slab_in.at[step, place],
                slab_send.at[step, place], slab_recv.at[step, place],
                device_id=device(SIDES[place]), device_id_type=MESH,
            )
            for place in range(2)
        ]

    def pack_copies(step):
        copies = []
        for place, side in enumerate(SIDES):
            begin, length = (0, 2) if place == 0 else (1, 2) if place == 1 else (1, 1)
            copies.append(
                pltpu.make_async_remote_copy(
                    pack_out.at[step, pl.ds(begin, length)],
                    pack_in.at[step, place, pl.ds(0, length)],
                    pack_send.at[step, place], pack_recv.at[step, place],
                    device_id=device(side), device_id_type=MESH,
                )
            )
        return copies

    def collide(step, own, store):
        grouped, inside, packed = own

        def from_side(side):
            if side == (0, 0):
                return packed
            place = SIDES.index((-side[0], -side[1]))
            return pack_in[step, place, 1 if place == 0 else 0]

        def pulled(kind, n, x):
            velocities, buf = (PHASE_VELOCITIES, h_buf) if kind == "h" else (FLOW_VELOCITIES, f_buf)
            cx, cy, cz = velocities[n]
            source = x - cx
            side = -1 if source < 0 else 1 if source >= nx else 0
            if side == 0:
                tile = buf[step, n, source]
            else:
                tile = slab_in[step, 0 if side == 1 else 1, CROSSING[-side].index((kind, n))]
            if cy:
                column = from_side((side, -cy))
                slot = slots[kind, n, source - side * nx]
                edge = 0 if cy == 1 else ny - 1
                tile = jnp.where(lanes == edge, turn(column, edge - slot, 1), turn(tile, cy, 1))
            return turn(tile, cz, 0)

        phase_read = [[pulled("h", n, x) for n in range(15)] for x in range(nx)]
        field = {x: functools.reduce(jnp.add, phase_read[x]) for x in range(nx)}

        def column_sum(kind, x, gy_side):
            total = None
            for side in (0, 1, -1):
                at = x - side * nx
                if -1 <= at <= nx:
                    value = turn(from_side((side, gy_side)), -slots[kind, at], 1)
                    total = value if total is None else total + value
            return total

        for x, edge_layer, side in ((-1, nx - 1, -1), (nx, 0, 1)):
            place = SIDES.index((-side, 0))
            value = inside[x] + pack_in[step, place, 0 if place == 0 else 1]
            for kind, gy_side, where in (("push+", -1, 0), ("push-", 1, ny - 1)):
                added = None
                for across in (0, side):
                    at = x - across * nx
                    term = turn(from_side((across, gy_side)), where - slots[kind, at], 1)
                    added = term if added is None else added + term
                value = value + jnp.where(lanes == where, added, 0.0)
            field[x] = value

        flat, sideways, steep, deep = {}, {}, {}, {}
        star = {}
        for x in range(-1, nx + 1):
            phi = field[x]
            before = column_sum("push-", x, 0) + column_sum("edge+", x, -1)
            after = turn(column_sum("push+", x, 0) + column_sum("edge-", x, 1), ny - 1, 1)
            left = jnp.where(first, before, turn(phi, 1, 1))
            right = jnp.where(last, after, turn(phi, -1, 1))
            above, below = up(phi), down(phi)
            flat[x] = left + right
            sideways[x] = right - left
            steep[x] = above - below
            deep[x] = above + below
            star[x] = 2.0 * phi + flat[x] + deep[x]

        for x in range(nx):
            phi = field[x]
            dy, ys = sideways[x], flat[x]
            ys_up, ys_down = up(ys), down(ys)
            dx_grad = (star[x + 1] - star[x - 1]) * (1.0 / 12.0)
            dy_grad = (2.0 * dy + sideways[x + 1] + sideways[x - 1] + up(dy) + down(dy)) * (1.0 / 12.0)
            dz_grad = (2.0 * steep[x] + steep[x + 1] + steep[x - 1] + ys_up - ys_down) * (1.0 / 12.0)
            ringed = star[x + 1] + star[x - 1] + 2.0 * (ys + deep[x]) + ys_up + ys_down
            laplacian = ringed * (1.0 / 6.0) - 4.0 * phi
            gradient = (dx_grad, dy_grad, dz_grad)
            squared = dx_grad * dx_grad + dy_grad * dy_grad + dz_grad * dz_grad
            scaling = lax.rsqrt(jnp.maximum(squared, GRADIENT_FLOOR * GRADIENT_FLOOR))
            clipped = jnp.clip(phi, 0.0, 1.0)
            inv_density = 1.0 / (1.0 + 2.0 * clipped)
            inv_time = 1.0 / (0.6 + 0.4 * clipped)
            potential = 4.0 * BETA * phi * (phi - 1.0) * (phi - 0.5) - KAPPA * laplacian
            force = [potential * component for component in gradient]
            read = [pulled("f", n, x) for n in range(19)]
            pressure = functools.reduce(jnp.add, read)
            velocity = []
            for coordinate in range(3):
                moment = 0.5 * force[coordinate]
                for n in range(19):
                    if FLOW_VELOCITIES[n][coordinate] == 1:
                        moment = moment + read[n]
                    elif FLOW_VELOCITIES[n][coordinate] == -1:
                        moment = moment - read[n]
                velocity.append(moment * inv_density)
            speed_sq = velocity[0] * velocity[0] + velocity[1] * velocity[1] + velocity[2] * velocity[2]
            force_factor = 3.0 * (1.0 - 0.5 * inv_time) * inv_density
            keep = 1.0 - inv_time
            drift = [3.0 * inv_time * velocity[k] + force_factor * force[k] for k in range(3)]
            level = inv_time * (pressure - 1.5 * speed_sq)
            curve = 4.5 * inv_time
            solid_cells = solid[x] > 0

            def along(vector, values):
                total = None
                for c, value in zip(vector, values):
                    if c == 0:
                        continue
                    if total is None:
                        total = value
                        assert c == 1
                    else:
                        total = total + value if c == 1 else total - value
                return total

            store("f", 0, x, jnp.where(solid_cells, read[0], read[0] * keep + FLOW_WEIGHTS[0] * level))
            for weight in sorted(set(FLOW_WEIGHTS[1:])):
                level_w, curve_w = weight * level, weight * curve
                drift_w = [weight * value for value in drift]
                for n in range(1, 19):
                    vector = FLOW_VELOCITIES[n]
                    if FLOW_WEIGHTS[n] != weight or [c for c in vector if c][0] != 1:
                        continue
                    m = opposite(FLOW_VELOCITIES, n)
                    speed = along(vector, velocity)
                    even = level_w + curve_w * (speed * speed)
                    odd = along(vector, drift_w)
                    store("f", n, x, jnp.where(solid_cells, read[m], read[n] * keep + (even + odd)))
                    store("f", m, x, jnp.where(solid_cells, read[n], read[m] * keep + (even - odd)))

            gain = 1.0 / PHASE_RELAX
            interface = PHASE_LAMBDA * phi * (1.0 - phi) * scaling
            tilt = [3.0 * phi * velocity[k] + interface * gradient[k] for k in range(3)]
            pops = phase_read[x]
            store("h", 0, x, jnp.where(solid_cells, pops[0], (1.0 - gain) * pops[0] + gain * PHASE_WEIGHTS[0] * phi))
            for weight in sorted(set(PHASE_WEIGHTS[1:])):
                phi_w = (gain * weight) * phi
                tilt_w = [(gain * weight) * value for value in tilt]
                for n in range(1, 15):
                    vector = PHASE_VELOCITIES[n]
                    if PHASE_WEIGHTS[n] != weight or [c for c in vector if c][0] != 1:
                        continue
                    m = opposite(PHASE_VELOCITIES, n)
                    odd = along(vector, tilt_w)
                    store("h", n, x, jnp.where(solid_cells, pops[m], (1.0 - gain) * pops[n] + (phi_w + odd)))
                    store("h", m, x, jnp.where(solid_cells, pops[n], (1.0 - gain) * pops[m] + (phi_w - odd)))

    for load in loads:
        load.wait()
    started = []
    for step in range(STEPS):
        fill_slab(step)
        if step == 0:
            own = pushes(step)
            pl.semaphore_wait(barrier, len(SIDES))
            packs, slabs = pack_copies(step), slab_copies(step)
            for copy in packs + slabs:
                copy.start()
        else:
            slabs = slab_copies(step)
            for copy in slabs:
                copy.start()
            own = pushes(step)
            packs = pack_copies(step)
            for copy in packs:
                copy.start()
        started += packs + slabs
        for copy in packs + slabs:
            copy.wait_recv()

        def store(kind, n, x, value):
            (h_buf if kind == "h" else f_buf)[step + 1, n, x] = value

        collide(step, own, store)
    stores = [
        pltpu.make_async_copy(h_buf.at[STEPS], phase_out, store_sem.at[0]),
        pltpu.make_async_copy(f_buf.at[STEPS], flow_out, store_sem.at[1]),
    ]
    for copy in stores:
        copy.start()
    for copy in started:
        copy.wait_send()
    for copy in stores:
        copy.wait()


def shards(size_gx, size_gy, phase_pops, flow_pops, solid_flags):
    nx, nz, ny = solid_flags.shape
    f32 = jnp.float32
    crossing = len(CROSSING[1])
    anywhere = pl.BlockSpec(memory_space=pl.ANY)
    return pl.pallas_call(
        functools.partial(kernel, size_gx, size_gy),
        out_shape=(
            jax.ShapeDtypeStruct(phase_pops.shape, f32),
            jax.ShapeDtypeStruct(flow_pops.shape, f32),
        ),
        in_specs=[anywhere] * 3,
        out_specs=(anywhere, anywhere),
        scratch_shapes=[
            pltpu.VMEM((STEPS + 1,) + phase_pops.shape, f32),
            pltpu.VMEM((STEPS + 1,) + flow_pops.shape, f32),
            pltpu.VMEM((nx, nz, ny), jnp.int32),
            pltpu.VMEM((STEPS, 2, crossing, nz, ny), f32),
            pltpu.VMEM((STEPS, 2, crossing, nz, ny), f32),
            pltpu.VMEM((STEPS, 3, nz, ny), f32),
            pltpu.VMEM((STEPS, len(SIDES), 2, nz, ny), f32),
            pltpu.SemaphoreType.DMA((3,)),
            pltpu.SemaphoreType.DMA((2,)),
            pltpu.SemaphoreType.DMA((STEPS, 2)),
            pltpu.SemaphoreType.DMA((STEPS, 2)),
            pltpu.SemaphoreType.DMA((STEPS, len(SIDES))),
            pltpu.SemaphoreType.DMA((STEPS, len(SIDES))),
        ],
        compiler_params=pltpu.CompilerParams(collective_id=0, has_side_effects=True),
    )(phase_pops, flow_pops, solid_flags)


def solution(mesh):
    placed = P(None, "gx", None, "gy")
    return jax.shard_map(
        functools.partial(shards, mesh.shape["gx"], mesh.shape["gy"]),
        mesh=mesh,
        in_specs=(placed, placed, P("gx", None, "gy")),
        out_specs=(placed, placed),
        check_vma=False,
    )
```

```python
import functools

import jax
import jax.numpy as jnp
from jax import lax
from jax.experimental import pallas as pl
from jax.experimental.pallas import tpu as pltpu
from jax.sharding import PartitionSpec as P

STEPS = 2
PHASE_VELOCITIES = [
    (0, 0, 0), (1, 0, 0), (-1, 0, 0), (0, 1, 0), (0, -1, 0), (0, 0, 1), (0, 0, -1),
    (1, 1, 1), (1, 1, -1), (1, -1, 1), (1, -1, -1),
    (-1, 1, 1), (-1, 1, -1), (-1, -1, 1), (-1, -1, -1),
]
PHASE_WEIGHTS = [2.0 / 9.0] + [1.0 / 9.0] * 6 + [1.0 / 72.0] * 8
FLOW_VELOCITIES = [
    (0, 0, 0), (1, 0, 0), (-1, 0, 0), (0, 1, 0), (0, -1, 0), (0, 0, 1), (0, 0, -1),
    (1, 1, 0), (1, -1, 0), (-1, 1, 0), (-1, -1, 0),
    (1, 0, 1), (1, 0, -1), (-1, 0, 1), (-1, 0, -1),
    (0, 1, 1), (0, 1, -1), (0, -1, 1), (0, -1, -1),
]
FLOW_WEIGHTS = [1.0 / 3.0] + [1.0 / 18.0] * 6 + [1.0 / 36.0] * 12
SURFACE_TENSION = 0.05
INTERFACE_WIDTH = 4.0
GRADIENT_FLOOR = 0.1
PHASE_LAMBDA = 0.3
PHASE_RELAX = 0.8
BETA = 12.0 * SURFACE_TENSION / INTERFACE_WIDTH
KAPPA = 1.5 * SURFACE_TENSION * INTERFACE_WIDTH

MESH = pl.DeviceIdType.MESH
SIDES = [(-1, 0), (1, 0), (0, -1), (0, 1), (-1, -1), (-1, 1), (1, -1), (1, 1)]


def moving(velocities, coordinate, sign):
    return [n for n, vector in enumerate(velocities) if vector[coordinate] == sign]


CROSSING = {
    sign: [("h", n) for n in moving(PHASE_VELOCITIES, 0, sign)]
    + [("f", n) for n in moving(FLOW_VELOCITIES, 0, sign)]
    for sign in (1, -1)
}


def opposite(velocities, n):
    vector = velocities[n]
    return velocities.index((-vector[0], -vector[1], -vector[2]))


def slot_table(nx):
    slots = {}
    for sign in (1, -1):
        for kind, velocities in (("h", PHASE_VELOCITIES), ("f", FLOW_VELOCITIES)):
            for n in moving(velocities, 1, sign):
                for x in range(nx):
                    slots[kind, n, x] = len(slots)
    for kind in ("edge+", "edge-", "push+", "push-"):
        for x in range(-1, nx + 1):
            slots[kind, x] = len(slots)
    return slots


def kernel(
    size_gx, size_gy, phase_in, flow_in, solid_in, phase_out, flow_out,
    h_buf, f_buf, solid, slab_out, slab_in, pack_out, pack_in,
    load_sem, slab_send, slab_recv, pack_send, pack_recv,
):
    nx, nz, ny = solid.shape
    slots = slot_table(nx)
    assert len(slots) <= ny
    gx, gy = lax.axis_index("gx"), lax.axis_index("gy")

    def device(side):
        return (lax.rem(gx + side[0] + size_gx, size_gx), lax.rem(gy + side[1] + size_gy, size_gy))

    loads = [
        pltpu.make_async_copy(phase_in, h_buf.at[0], load_sem.at[0]),
        pltpu.make_async_copy(flow_in, f_buf.at[0], load_sem.at[1]),
        pltpu.make_async_copy(solid_in, solid, load_sem.at[2]),
    ]
    for load in loads:
        load.start()
    barrier = pltpu.get_barrier_semaphore()
    for side in SIDES:
        pl.semaphore_signal(barrier, inc=1, device_id=device(side), device_id_type=MESH)

    lanes = lax.broadcasted_iota(jnp.int32, (nz, ny), 1)
    first, last = lanes == 0, lanes == ny - 1

    def turn(tile, shift, axis):
        shift %= tile.shape[axis]
        return pltpu.roll(tile, shift, axis) if shift else tile

    def up(tile):
        return turn(tile, -1, 0)

    def down(tile):
        return turn(tile, 1, 0)

    def pushes(step):
        grouped = {}
        for x in range(nx):
            for n, (cx, cy, cz) in enumerate(PHASE_VELOCITIES):
                value = turn(h_buf[step, n, x], cz, 0)
                key = (cy, x + cx)
                grouped[key] = grouped[key] + value if key in grouped else value
        inside = {}
        for x in range(-1, nx + 1):
            inside[x] = (
                grouped[0, x]
                + jnp.where(first, 0.0, turn(grouped[1, x], 1, 1))
                + jnp.where(last, 0.0, turn(grouped[-1, x], -1, 1))
            )
        packed = jnp.zeros((nz, ny), jnp.float32)
        for key, slot in slots.items():
            if key[0] in ("h", "f"):
                kind, n, x = key
                velocities, buf = (PHASE_VELOCITIES, h_buf) if kind == "h" else (FLOW_VELOCITIES, f_buf)
                sign, tile = velocities[n][1], buf[step, n, x]
            else:
                sign = 1 if key[0][-1] == "+" else -1
                tile = inside[key[1]] if key[0][:4] == "edge" else grouped[sign, key[1]]
            source = ny - 1 if sign == 1 else 0
            packed = jnp.where(lanes == slot, turn(tile, slot - source, 1), packed)
        pack_out[step, 0] = inside[0]
        pack_out[step, 1] = packed
        pack_out[step, 2] = inside[nx - 1]
        return grouped, inside, packed

    def fill_slab(step):
        for place, sign in enumerate((-1, 1)):
            x = 0 if sign == -1 else nx - 1
            for k, (kind, n) in enumerate(CROSSING[sign]):
                slab_out[step, place, k] = (h_buf if kind == "h" else f_buf)[step, n, x]

    def slab_copies(step):
        return [
            pltpu.make_async_remote_copy(
                slab_out.at[step, place], slab_in.at[step, place],
                slab_send.at[step, place], slab_recv.at[step, place],
                device_id=device(SIDES[place]), device_id_type=MESH,
            )
            for place in range(2)
        ]

    def pack_copies(step):
        copies = []
        for place, side in enumerate(SIDES):
            begin, length = (0, 2) if place == 0 else (1, 2) if place == 1 else (1, 1)
            copies.append(
                pltpu.make_async_remote_copy(
                    pack_out.at[step, pl.ds(begin, length)],
                    pack_in.at[step, place, pl.ds(0, length)],
                    pack_send.at[step, place], pack_recv.at[step, place],
                    device_id=device(side), device_id_type=MESH,
                )
            )
        return copies

    def collide(step, own, store):
        grouped, inside, packed = own

        def from_side(side):
            if side == (0, 0):
                return packed
            place = SIDES.index((-side[0], -side[1]))
            return pack_in[step, place, 1 if place == 0 else 0]

        def pulled(kind, n, x):
            velocities, buf = (PHASE_VELOCITIES, h_buf) if kind == "h" else (FLOW_VELOCITIES, f_buf)
            cx, cy, cz = velocities[n]
            source = x - cx
            side = -1 if source < 0 else 1 if source >= nx else 0
            if side == 0:
                tile = buf[step, n, source]
            else:
                tile = slab_in[step, 0 if side == 1 else 1, CROSSING[-side].index((kind, n))]
            if cy:
                column = from_side((side, -cy))
                slot = slots[kind, n, source - side * nx]
                edge = 0 if cy == 1 else ny - 1
                tile = jnp.where(lanes == edge, turn(column, edge - slot, 1), turn(tile, cy, 1))
            return turn(tile, cz, 0)

        phase_read = [[pulled("h", n, x) for n in range(15)] for x in range(nx)]
        field = {x: functools.reduce(jnp.add, phase_read[x]) for x in range(nx)}

        def column_sum(kind, x, gy_side):
            total = None
            for side in (0, 1, -1):
                at = x - side * nx
                if -1 <= at <= nx:
                    value = turn(from_side((side, gy_side)), -slots[kind, at], 1)
                    total = value if total is None else total + value
            return total

        for x, edge_layer, side in ((-1, nx - 1, -1), (nx, 0, 1)):
            place = SIDES.index((-side, 0))
            value = inside[x] + pack_in[step, place, 0 if place == 0 else 1]
            for kind, gy_side, where in (("push+", -1, 0), ("push-", 1, ny - 1)):
                added = None
                for across in (0, side):
                    at = x - across * nx
                    term = turn(from_side((across, gy_side)), where - slots[kind, at], 1)
                    added = term if added is None else added + term
                value = value + jnp.where(lanes == where, added, 0.0)
            field[x] = value

        flat, sideways, steep, deep = {}, {}, {}, {}
        star = {}
        for x in range(-1, nx + 1):
            phi = field[x]
            before = column_sum("push-", x, 0) + column_sum("edge+", x, -1)
            after = turn(column_sum("push+", x, 0) + column_sum("edge-", x, 1), ny - 1, 1)
            left = jnp.where(first, before, turn(phi, 1, 1))
            right = jnp.where(last, after, turn(phi, -1, 1))
            above, below = up(phi), down(phi)
            flat[x] = left + right
            sideways[x] = right - left
            steep[x] = above - below
            deep[x] = above + below
            star[x] = 2.0 * phi + flat[x] + deep[x]

        for x in range(nx):
            phi = field[x]
            dy, ys = sideways[x], flat[x]
            ys_up, ys_down = up(ys), down(ys)
            dx_grad = (star[x + 1] - star[x - 1]) * (1.0 / 12.0)
            dy_grad = (2.0 * dy + sideways[x + 1] + sideways[x - 1] + up(dy) + down(dy)) * (1.0 / 12.0)
            dz_grad = (2.0 * steep[x] + steep[x + 1] + steep[x - 1] + ys_up - ys_down) * (1.0 / 12.0)
            ringed = star[x + 1] + star[x - 1] + 2.0 * (ys + deep[x]) + ys_up + ys_down
            laplacian = ringed * (1.0 / 6.0) - 4.0 * phi
            gradient = (dx_grad, dy_grad, dz_grad)
            squared = dx_grad * dx_grad + dy_grad * dy_grad + dz_grad * dz_grad
            scaling = lax.rsqrt(jnp.maximum(squared, GRADIENT_FLOOR * GRADIENT_FLOOR))
            clipped = jnp.clip(phi, 0.0, 1.0)
            inv_density = 1.0 / (1.0 + 2.0 * clipped)
            inv_time = 1.0 / (0.6 + 0.4 * clipped)
            potential = 4.0 * BETA * phi * (phi - 1.0) * (phi - 0.5) - KAPPA * laplacian
            force = [potential * component for component in gradient]
            read = [pulled("f", n, x) for n in range(19)]
            pressure = functools.reduce(jnp.add, read)
            velocity = []
            for coordinate in range(3):
                moment = 0.5 * force[coordinate]
                for n in range(19):
                    if FLOW_VELOCITIES[n][coordinate] == 1:
                        moment = moment + read[n]
                    elif FLOW_VELOCITIES[n][coordinate] == -1:
                        moment = moment - read[n]
                velocity.append(moment * inv_density)
            speed_sq = velocity[0] * velocity[0] + velocity[1] * velocity[1] + velocity[2] * velocity[2]
            force_factor = 3.0 * (1.0 - 0.5 * inv_time) * inv_density
            keep = 1.0 - inv_time
            drift = [3.0 * inv_time * velocity[k] + force_factor * force[k] for k in range(3)]
            level = inv_time * (pressure - 1.5 * speed_sq)
            curve = 4.5 * inv_time
            solid_cells = solid[x] > 0

            def along(vector, values):
                total = None
                for c, value in zip(vector, values):
                    if c == 0:
                        continue
                    if total is None:
                        total = value
                        assert c == 1
                    else:
                        total = total + value if c == 1 else total - value
                return total

            store("f", 0, x, jnp.where(solid_cells, read[0], read[0] * keep + FLOW_WEIGHTS[0] * level))
            for weight in sorted(set(FLOW_WEIGHTS[1:])):
                level_w, curve_w = weight * level, weight * curve
                drift_w = [weight * value for value in drift]
                for n in range(1, 19):
                    vector = FLOW_VELOCITIES[n]
                    if FLOW_WEIGHTS[n] != weight or [c for c in vector if c][0] != 1:
                        continue
                    m = opposite(FLOW_VELOCITIES, n)
                    speed = along(vector, velocity)
                    even = level_w + curve_w * (speed * speed)
                    odd = along(vector, drift_w)
                    store("f", n, x, jnp.where(solid_cells, read[m], read[n] * keep + (even + odd)))
                    store("f", m, x, jnp.where(solid_cells, read[n], read[m] * keep + (even - odd)))

            gain = 1.0 / PHASE_RELAX
            interface = PHASE_LAMBDA * phi * (1.0 - phi) * scaling
            tilt = [3.0 * phi * velocity[k] + interface * gradient[k] for k in range(3)]
            pops = phase_read[x]
            store("h", 0, x, jnp.where(solid_cells, pops[0], (1.0 - gain) * pops[0] + gain * PHASE_WEIGHTS[0] * phi))
            for weight in sorted(set(PHASE_WEIGHTS[1:])):
                phi_w = (gain * weight) * phi
                tilt_w = [(gain * weight) * value for value in tilt]
                for n in range(1, 15):
                    vector = PHASE_VELOCITIES[n]
                    if PHASE_WEIGHTS[n] != weight or [c for c in vector if c][0] != 1:
                        continue
                    m = opposite(PHASE_VELOCITIES, n)
                    odd = along(vector, tilt_w)
                    store("h", n, x, jnp.where(solid_cells, pops[m], (1.0 - gain) * pops[n] + (phi_w + odd)))
                    store("h", m, x, jnp.where(solid_cells, pops[n], (1.0 - gain) * pops[m] + (phi_w - odd)))

    for load in loads:
        load.wait()
    started = []
    for step in range(STEPS):
        fill_slab(step)
        if step == 0:
            own = pushes(step)
            pl.semaphore_wait(barrier, len(SIDES))
            packs, slabs = pack_copies(step), slab_copies(step)
            for copy in packs + slabs:
                copy.start()
        else:
            slabs = slab_copies(step)
            for copy in slabs:
                copy.start()
            own = pushes(step)
            packs = pack_copies(step)
            for copy in packs:
                copy.start()
        started += packs + slabs
        for copy in packs + slabs:
            copy.wait_recv()

        def store(kind, n, x, value):
            if step + 1 == STEPS:
                (phase_out if kind == "h" else flow_out)[n, x] = value
            else:
                (h_buf if kind == "h" else f_buf)[step + 1, n, x] = value

        collide(step, own, store)
    for copy in started:
        copy.wait_send()


def write_back(phase, flow, phase_out, flow_out, sems):
    copies = [
        pltpu.make_async_copy(phase, phase_out, sems.at[0]),
        pltpu.make_async_copy(flow, flow_out, sems.at[1]),
    ]
    for copy in copies:
        copy.start()
    for copy in copies:
        copy.wait()


def shards(size_gx, size_gy, phase_pops, flow_pops, solid_flags):
    nx, nz, ny = solid_flags.shape
    f32 = jnp.float32
    crossing = len(CROSSING[1])
    anywhere = pl.BlockSpec(memory_space=pl.ANY)
    shapes = (phase_pops.shape, flow_pops.shape)
    on_chip = pl.BlockSpec(memory_space=pltpu.VMEM)
    results = pl.pallas_call(
        functools.partial(kernel, size_gx, size_gy),
        out_shape=tuple(pltpu.VMEM(shape, f32) for shape in shapes),
        in_specs=[anywhere] * 3,
        out_specs=(on_chip, on_chip),
        scratch_shapes=[
            pltpu.VMEM((STEPS,) + phase_pops.shape, f32),
            pltpu.VMEM((STEPS,) + flow_pops.shape, f32),
            pltpu.VMEM((nx, nz, ny), jnp.int32),
            pltpu.VMEM((STEPS, 2, crossing, nz, ny), f32),
            pltpu.VMEM((STEPS, 2, crossing, nz, ny), f32),
            pltpu.VMEM((STEPS, 3, nz, ny), f32),
            pltpu.VMEM((STEPS, len(SIDES), 2, nz, ny), f32),
            pltpu.SemaphoreType.DMA((3,)),
            pltpu.SemaphoreType.DMA((STEPS, 2)),
            pltpu.SemaphoreType.DMA((STEPS, 2)),
            pltpu.SemaphoreType.DMA((STEPS, len(SIDES))),
            pltpu.SemaphoreType.DMA((STEPS, len(SIDES))),
        ],
        compiler_params=pltpu.CompilerParams(collective_id=0, has_side_effects=True),
    )(phase_pops, flow_pops, solid_flags)
    return pl.pallas_call(
        write_back,
        out_shape=tuple(jax.ShapeDtypeStruct(shape, f32) for shape in shapes),
        in_specs=[on_chip, on_chip],
        out_specs=(anywhere, anywhere),
        scratch_shapes=[pltpu.SemaphoreType.DMA((2,))],
    )(*[pltpu.with_memory_space_constraint(r, pltpu.VMEM) for r in results])


def solution(mesh):
    placed = P(None, "gx", None, "gy")
    return jax.shard_map(
        functools.partial(shards, mesh.shape["gx"], mesh.shape["gy"]),
        mesh=mesh,
        in_specs=(placed, placed, P("gx", None, "gy")),
        out_specs=(placed, placed),
        check_vma=False,
    )
```

```python
import functools

import jax
import jax.numpy as jnp
from jax import lax
from jax.experimental import pallas as pl
from jax.experimental.pallas import tpu as pltpu
from jax.sharding import PartitionSpec as P

STEPS = 2
PHASE_VELOCITIES = [
    (0, 0, 0), (1, 0, 0), (-1, 0, 0), (0, 1, 0), (0, -1, 0), (0, 0, 1), (0, 0, -1),
    (1, 1, 1), (1, 1, -1), (1, -1, 1), (1, -1, -1),
    (-1, 1, 1), (-1, 1, -1), (-1, -1, 1), (-1, -1, -1),
]
PHASE_WEIGHTS = [2.0 / 9.0] + [1.0 / 9.0] * 6 + [1.0 / 72.0] * 8
FLOW_VELOCITIES = [
    (0, 0, 0), (1, 0, 0), (-1, 0, 0), (0, 1, 0), (0, -1, 0), (0, 0, 1), (0, 0, -1),
    (1, 1, 0), (1, -1, 0), (-1, 1, 0), (-1, -1, 0),
    (1, 0, 1), (1, 0, -1), (-1, 0, 1), (-1, 0, -1),
    (0, 1, 1), (0, 1, -1), (0, -1, 1), (0, -1, -1),
]
FLOW_WEIGHTS = [1.0 / 3.0] + [1.0 / 18.0] * 6 + [1.0 / 36.0] * 12
SURFACE_TENSION = 0.05
INTERFACE_WIDTH = 4.0
GRADIENT_FLOOR = 0.1
PHASE_LAMBDA = 0.3
PHASE_RELAX = 0.8
BETA = 12.0 * SURFACE_TENSION / INTERFACE_WIDTH
KAPPA = 1.5 * SURFACE_TENSION * INTERFACE_WIDTH

MESH = pl.DeviceIdType.MESH
SIDES = [(-1, 0), (1, 0), (0, -1), (0, 1), (-1, -1), (-1, 1), (1, -1), (1, 1)]


def moving(velocities, coordinate, sign):
    return [n for n, vector in enumerate(velocities) if vector[coordinate] == sign]


CROSSING = {
    sign: [("h", n) for n in moving(PHASE_VELOCITIES, 0, sign)]
    + [("f", n) for n in moving(FLOW_VELOCITIES, 0, sign)]
    for sign in (1, -1)
}


def opposite(velocities, n):
    vector = velocities[n]
    return velocities.index((-vector[0], -vector[1], -vector[2]))


def slot_table(nx):
    slots = {}
    for sign in (1, -1):
        for kind, velocities in (("h", PHASE_VELOCITIES), ("f", FLOW_VELOCITIES)):
            for n in moving(velocities, 1, sign):
                for x in range(nx):
                    slots[kind, n, x] = len(slots)
    for kind in ("edge+", "edge-", "push+", "push-"):
        for x in range(-1, nx + 1):
            slots[kind, x] = len(slots)
    return slots


def kernel(
    size_gx, size_gy, phase_in, flow_in, solid_in, phase_out, flow_out,
    h_buf, f_buf, h_moved, f_moved, solid, slab_out, slab_in, pack_out, pack_in,
    load_sem, slab_send, slab_recv, pack_send, pack_recv,
):
    nx, nz, ny = solid.shape
    slots = slot_table(nx)
    assert len(slots) <= ny
    gx, gy = lax.axis_index("gx"), lax.axis_index("gy")

    def device(side):
        return (lax.rem(gx + side[0] + size_gx, size_gx), lax.rem(gy + side[1] + size_gy, size_gy))

    barrier = pltpu.get_barrier_semaphore()
    for side in reversed(SIDES):
        pl.semaphore_signal(barrier, inc=1, device_id=device(side), device_id_type=MESH)
    loads = [
        pltpu.make_async_copy(phase_in, h_buf.at[0], load_sem.at[0]),
        pltpu.make_async_copy(flow_in, f_buf.at[0], load_sem.at[1]),
        pltpu.make_async_copy(solid_in, solid, load_sem.at[2]),
    ]
    for load in loads:
        load.start()

    lanes = lax.broadcasted_iota(jnp.int32, (nz, ny), 1)
    first, last = lanes == 0, lanes == ny - 1

    def turn(tile, shift, axis):
        shift %= tile.shape[axis]
        return pltpu.roll(tile, shift, axis) if shift else tile

    def up(tile):
        return turn(tile, -1, 0)

    def down(tile):
        return turn(tile, 1, 0)

    def pushes(step):
        grouped = {}
        for x in range(nx):
            for n, (cx, cy, cz) in enumerate(PHASE_VELOCITIES):
                value = turn(h_buf[step, n, x], cz, 0)
                key = (cy, x + cx)
                grouped[key] = grouped[key] + value if key in grouped else value
        inside = {}
        for x in range(-1, nx + 1):
            inside[x] = (
                grouped[0, x]
                + jnp.where(first, 0.0, turn(grouped[1, x], 1, 1))
                + jnp.where(last, 0.0, turn(grouped[-1, x], -1, 1))
            )
        packed = jnp.zeros((nz, ny), jnp.float32)
        for key, slot in slots.items():
            if key[0] in ("h", "f"):
                kind, n, x = key
                velocities, buf = (PHASE_VELOCITIES, h_buf) if kind == "h" else (FLOW_VELOCITIES, f_buf)
                sign, tile = velocities[n][1], buf[step, n, x]
            else:
                sign = 1 if key[0][-1] == "+" else -1
                tile = inside[key[1]] if key[0][:4] == "edge" else grouped[sign, key[1]]
            source = ny - 1 if sign == 1 else 0
            packed = jnp.where(lanes == slot, turn(tile, slot - source, 1), packed)
        pack_out[step, 0] = inside[0]
        pack_out[step, 1] = packed
        pack_out[step, 2] = inside[nx - 1]
        return grouped, inside, packed

    def fill_slab(step):
        for place, sign in enumerate((-1, 1)):
            x = 0 if sign == -1 else nx - 1
            for k, (kind, n) in enumerate(CROSSING[sign]):
                slab_out[step, place, k] = (h_buf if kind == "h" else f_buf)[step, n, x]

    def slab_copies(step):
        return [
            pltpu.make_async_remote_copy(
                slab_out.at[step, place], slab_in.at[step, place],
                slab_send.at[step, place], slab_recv.at[step, place],
                device_id=device(SIDES[place]), device_id_type=MESH,
            )
            for place in range(2)
        ]

    def pack_copies(step):
        copies = []
        for place, side in enumerate(SIDES):
            begin, length = (0, 2) if place == 0 else (1, 2) if place == 1 else (1, 1)
            copies.append(
                pltpu.make_async_remote_copy(
                    pack_out.at[step, pl.ds(begin, length)],
                    pack_in.at[step, place, pl.ds(0, length)],
                    pack_send.at[step, place], pack_recv.at[step, place],
                    device_id=device(side), device_id_type=MESH,
                )
            )
        return copies

    tables = {"h": (PHASE_VELOCITIES, h_buf, h_moved), "f": (FLOW_VELOCITIES, f_buf, f_moved)}

    def origin(step, kind, n, x):
        velocities, buf, _ = tables[kind]
        source = x - velocities[n][0]
        side = -1 if source < 0 else 1 if source >= nx else 0
        if side == 0:
            return source, side, buf[step, n, source]
        return source, side, slab_in[step, 0 if side == 1 else 1, CROSSING[-side].index((kind, n))]

    def stage(step, from_slab):
        for kind, (velocities, _, moved) in tables.items():
            for n, (cx, cy, cz) in enumerate(velocities):
                for x in range(nx):
                    if (cy or cz) and (0 <= x - cx < nx) != from_slab:
                        tile = origin(step, kind, n, x)[2]
                        moved[n, x] = turn(turn(tile, cy, 1), cz, 0)

    def collide(step, own, store):
        grouped, inside, packed = own

        def from_side(side):
            if side == (0, 0):
                return packed
            place = SIDES.index((-side[0], -side[1]))
            return pack_in[step, place, 1 if place == 0 else 0]

        def pulled(kind, n, x):
            velocities, buf, moved = tables[kind]
            cx, cy, cz = velocities[n]
            source, side, tile = origin(step, kind, n, x)
            if cy or cz:
                tile = moved[n, x]
            if cy:
                column = turned_side((side, -cy), cz)
                slot = slots[kind, n, source - side * nx]
                edge = 0 if cy == 1 else ny - 1
                tile = jnp.where(lanes == edge, turn(column, edge - slot, 1), tile)
            return tile

        turned = {}

        def turned_side(side, cz):
            if (side, cz) not in turned:
                turned[side, cz] = turn(from_side(side), cz, 0)
            return turned[side, cz]

        phase_read = [[pulled("h", n, x) for n in range(15)] for x in range(nx)]
        flat_first = sorted(range(15), key=lambda n: abs(PHASE_VELOCITIES[n][1]))
        field = {x: functools.reduce(jnp.add, [phase_read[x][n] for n in flat_first]) for x in range(nx)}

        def column_sum(kind, x, gy_side):
            total = None
            for side in (0, 1, -1):
                at = x - side * nx
                if -1 <= at <= nx:
                    value = turn(from_side((side, gy_side)), -slots[kind, at], 1)
                    total = value if total is None else total + value
            return total

        for x, edge_layer, side in ((-1, nx - 1, -1), (nx, 0, 1)):
            place = SIDES.index((-side, 0))
            value = inside[x] + pack_in[step, place, 0 if place == 0 else 1]
            for kind, gy_side, where in (("push+", -1, 0), ("push-", 1, ny - 1)):
                added = None
                for across in (0, side):
                    at = x - across * nx
                    term = turn(from_side((across, gy_side)), where - slots[kind, at], 1)
                    added = term if added is None else added + term
                value = value + jnp.where(lanes == where, added, 0.0)
            field[x] = value

        flat, sideways, steep, deep = {}, {}, {}, {}
        star = {}
        for x in range(-1, nx + 1):
            phi = field[x]
            before = column_sum("push-", x, 0) + column_sum("edge+", x, -1)
            after = turn(column_sum("push+", x, 0) + column_sum("edge-", x, 1), ny - 1, 1)
            left = jnp.where(first, before, turn(phi, 1, 1))
            right = jnp.where(last, after, turn(phi, -1, 1))
            above, below = up(phi), down(phi)
            flat[x] = left + right
            sideways[x] = right - left
            steep[x] = above - below
            deep[x] = above + below
            star[x] = 2.0 * phi + flat[x] + deep[x]

        for x in range(nx):
            phi = field[x]
            dy, ys = sideways[x], flat[x]
            ys_up, ys_down = up(ys), down(ys)
            dx_grad = (star[x + 1] - star[x - 1]) * (1.0 / 12.0)
            dy_grad = (2.0 * dy + sideways[x + 1] + sideways[x - 1] + up(dy) + down(dy)) * (1.0 / 12.0)
            dz_grad = (2.0 * steep[x] + steep[x + 1] + steep[x - 1] + ys_up - ys_down) * (1.0 / 12.0)
            ringed = star[x + 1] + star[x - 1] + 2.0 * (ys + deep[x]) + ys_up + ys_down
            laplacian = ringed * (1.0 / 6.0) - 4.0 * phi
            gradient = (dx_grad, dy_grad, dz_grad)
            squared = dx_grad * dx_grad + dy_grad * dy_grad + dz_grad * dz_grad
            scaling = lax.rsqrt(jnp.maximum(squared, GRADIENT_FLOOR * GRADIENT_FLOOR))
            clipped = jnp.clip(phi, 0.0, 1.0)
            inv_density = 1.0 / (1.0 + 2.0 * clipped)
            inv_time = 1.0 / (0.6 + 0.4 * clipped)
            potential = 4.0 * BETA * phi * (phi - 1.0) * (phi - 0.5) - KAPPA * laplacian
            force = [potential * component for component in gradient]
            read = [pulled("f", n, x) for n in range(19)]
            pressure = functools.reduce(jnp.add, read)
            velocity = []
            for coordinate in range(3):
                moment = 0.5 * force[coordinate]
                for n in range(19):
                    if FLOW_VELOCITIES[n][coordinate] == 1:
                        moment = moment + read[n]
                    elif FLOW_VELOCITIES[n][coordinate] == -1:
                        moment = moment - read[n]
                velocity.append(moment * inv_density)
            speed_sq = velocity[0] * velocity[0] + velocity[1] * velocity[1] + velocity[2] * velocity[2]
            force_factor = 3.0 * (1.0 - 0.5 * inv_time) * inv_density
            keep = 1.0 - inv_time
            drift = [3.0 * inv_time * velocity[k] + force_factor * force[k] for k in range(3)]
            level = inv_time * (pressure - 1.5 * speed_sq)
            curve = 4.5 * inv_time
            solid_cells = solid[x] > 0

            def along(vector, values):
                total = None
                for c, value in zip(vector, values):
                    if c == 0:
                        continue
                    if total is None:
                        total = value
                        assert c == 1
                    else:
                        total = total + value if c == 1 else total - value
                return total

            store("f", 0, x, jnp.where(solid_cells, read[0], read[0] * keep + FLOW_WEIGHTS[0] * level))
            for weight in sorted(set(FLOW_WEIGHTS[1:])):
                level_w, curve_w = weight * level, weight * curve
                drift_w = [weight * value for value in drift]
                for n in range(1, 19):
                    vector = FLOW_VELOCITIES[n]
                    if FLOW_WEIGHTS[n] != weight or [c for c in vector if c][0] != 1:
                        continue
                    m = opposite(FLOW_VELOCITIES, n)
                    speed = along(vector, velocity)
                    even = level_w + curve_w * (speed * speed)
                    odd = along(vector, drift_w)
                    store("f", n, x, jnp.where(solid_cells, read[m], read[n] * keep + (even + odd)))
                    store("f", m, x, jnp.where(solid_cells, read[n], read[m] * keep + (even - odd)))

            gain = 1.0 / PHASE_RELAX
            interface = PHASE_LAMBDA * phi * (1.0 - phi) * scaling
            tilt = [3.0 * phi * velocity[k] + interface * gradient[k] for k in range(3)]
            pops = phase_read[x]
            store("h", 0, x, jnp.where(solid_cells, pops[0], (1.0 - gain) * pops[0] + gain * PHASE_WEIGHTS[0] * phi))
            for weight in sorted(set(PHASE_WEIGHTS[1:])):
                phi_w = (gain * weight) * phi
                tilt_w = [(gain * weight) * value for value in tilt]
                for n in range(1, 15):
                    vector = PHASE_VELOCITIES[n]
                    if PHASE_WEIGHTS[n] != weight or [c for c in vector if c][0] != 1:
                        continue
                    m = opposite(PHASE_VELOCITIES, n)
                    odd = along(vector, tilt_w)
                    store("h", n, x, jnp.where(solid_cells, pops[m], (1.0 - gain) * pops[n] + (phi_w + odd)))
                    store("h", m, x, jnp.where(solid_cells, pops[n], (1.0 - gain) * pops[m] + (phi_w - odd)))

    for load in loads:
        load.wait()
    for step in range(STEPS):
        own = pushes(step)
        if step == 0:
            fill_slab(step)
            pl.semaphore_wait(barrier, len(SIDES))
        packs = pack_copies(step)
        for copy in reversed(packs):
            copy.start()
        if step > 0:
            fill_slab(step)
        slabs = slab_copies(step)
        for copy in slabs:
            copy.start()
        stage(step, False)
        for copy in packs + slabs:
            copy.wait_send()
        for copy in slabs:
            copy.wait_recv()
        stage(step, True)
        for copy in packs:
            copy.wait_recv()

        def store(kind, n, x, value):
            if step + 1 == STEPS:
                (phase_out if kind == "h" else flow_out)[n, x] = value
            else:
                (h_buf if kind == "h" else f_buf)[step + 1, n, x] = value

        collide(step, own, store)


def write_back(phase, flow, phase_out, flow_out, sems):
    copies = [
        pltpu.make_async_copy(phase, phase_out, sems.at[0]),
        pltpu.make_async_copy(flow, flow_out, sems.at[1]),
    ]
    for copy in copies:
        copy.start()
    for copy in copies:
        copy.wait()


def shards(size_gx, size_gy, phase_pops, flow_pops, solid_flags):
    nx, nz, ny = solid_flags.shape
    f32 = jnp.float32
    crossing = len(CROSSING[1])
    anywhere = pl.BlockSpec(memory_space=pl.ANY)
    shapes = (phase_pops.shape, flow_pops.shape)
    on_chip = pl.BlockSpec(memory_space=pltpu.VMEM)
    results = pl.pallas_call(
        functools.partial(kernel, size_gx, size_gy),
        out_shape=tuple(pltpu.VMEM(shape, f32) for shape in shapes),
        in_specs=[anywhere] * 3,
        out_specs=(on_chip, on_chip),
        scratch_shapes=[
            pltpu.VMEM((STEPS,) + phase_pops.shape, f32),
            pltpu.VMEM((STEPS,) + flow_pops.shape, f32),
            pltpu.VMEM(phase_pops.shape, f32),
            pltpu.VMEM(flow_pops.shape, f32),
            pltpu.VMEM((nx, nz, ny), jnp.int32),
            pltpu.VMEM((STEPS, 2, crossing, nz, ny), f32),
            pltpu.VMEM((STEPS, 2, crossing, nz, ny), f32),
            pltpu.VMEM((STEPS, 3, nz, ny), f32),
            pltpu.VMEM((STEPS, len(SIDES), 2, nz, ny), f32),
            pltpu.SemaphoreType.DMA((3,)),
            pltpu.SemaphoreType.DMA((STEPS, 2)),
            pltpu.SemaphoreType.DMA((STEPS, 2)),
            pltpu.SemaphoreType.DMA((STEPS, len(SIDES))),
            pltpu.SemaphoreType.DMA((STEPS, len(SIDES))),
        ],
        compiler_params=pltpu.CompilerParams(collective_id=0, has_side_effects=True),
    )(phase_pops, flow_pops, solid_flags)
    return pl.pallas_call(
        write_back,
        out_shape=tuple(jax.ShapeDtypeStruct(shape, f32) for shape in shapes),
        in_specs=[on_chip, on_chip],
        out_specs=(anywhere, anywhere),
        scratch_shapes=[pltpu.SemaphoreType.DMA((2,))],
    )(*[pltpu.with_memory_space_constraint(r, pltpu.VMEM) for r in results])


def solution(mesh):
    placed = P(None, "gx", None, "gy")
    return jax.shard_map(
        functools.partial(shards, mesh.shape["gx"], mesh.shape["gy"]),
        mesh=mesh,
        in_specs=(placed, placed, P("gx", None, "gy")),
        out_specs=(placed, placed),
        check_vma=False,
    )
```

```python
import functools

import jax
import jax.numpy as jnp
from jax import lax
from jax.experimental import pallas as pl
from jax.experimental.pallas import tpu as pltpu
from jax.sharding import PartitionSpec as P

STEPS = 2
PHASE_VELOCITIES = [
    (0, 0, 0), (1, 0, 0), (-1, 0, 0), (0, 1, 0), (0, -1, 0), (0, 0, 1), (0, 0, -1),
    (1, 1, 1), (1, 1, -1), (1, -1, 1), (1, -1, -1),
    (-1, 1, 1), (-1, 1, -1), (-1, -1, 1), (-1, -1, -1),
]
PHASE_WEIGHTS = [2.0 / 9.0] + [1.0 / 9.0] * 6 + [1.0 / 72.0] * 8
FLOW_VELOCITIES = [
    (0, 0, 0), (1, 0, 0), (-1, 0, 0), (0, 1, 0), (0, -1, 0), (0, 0, 1), (0, 0, -1),
    (1, 1, 0), (1, -1, 0), (-1, 1, 0), (-1, -1, 0),
    (1, 0, 1), (1, 0, -1), (-1, 0, 1), (-1, 0, -1),
    (0, 1, 1), (0, 1, -1), (0, -1, 1), (0, -1, -1),
]
FLOW_WEIGHTS = [1.0 / 3.0] + [1.0 / 18.0] * 6 + [1.0 / 36.0] * 12
SURFACE_TENSION = 0.05
INTERFACE_WIDTH = 4.0
GRADIENT_FLOOR = 0.1
PHASE_LAMBDA = 0.3
PHASE_RELAX = 0.8
BETA = 12.0 * SURFACE_TENSION / INTERFACE_WIDTH
KAPPA = 1.5 * SURFACE_TENSION * INTERFACE_WIDTH

MESH = pl.DeviceIdType.MESH
SIDES = [(-1, 0), (1, 0), (0, -1), (0, 1), (-1, -1), (-1, 1), (1, -1), (1, 1)]


def moving(velocities, coordinate, sign):
    return [n for n, vector in enumerate(velocities) if vector[coordinate] == sign]


CROSSING = {
    sign: [("h", n) for n in moving(PHASE_VELOCITIES, 0, sign)]
    + [("f", n) for n in moving(FLOW_VELOCITIES, 0, sign)]
    for sign in (1, -1)
}


def opposite(velocities, n):
    vector = velocities[n]
    return velocities.index((-vector[0], -vector[1], -vector[2]))


def slot_table(nx):
    slots = {}
    for sign, mark in ((1, "+"), (-1, "-")):
        keys = []
        for kind, velocities in (("h", PHASE_VELOCITIES), ("f", FLOW_VELOCITIES)):
            keys += [(kind, n, x) for n in moving(velocities, 1, sign) for x in range(nx)]
        for kind in ("edge", "push"):
            keys += [(kind + mark, x) for x in range(-1, nx + 1)]
        slots.update({key: slot for slot, key in enumerate(keys)})
    return slots


def kernel(
    size_gx, size_gy, phase_in, flow_in, solid_in, phase_out, flow_out,
    h_buf, f_buf, h_moved, f_moved, solid, slab_out, slab_in, pack_out, pack_in,
    load_sem, slab_send, slab_recv, pack_send, pack_recv,
):
    nx, nz, ny = solid.shape
    slots = slot_table(nx)
    half, fold = nz // 2, ny // 2
    assert max(slots.values()) < fold
    gx, gy = lax.axis_index("gx"), lax.axis_index("gy")

    def device(side):
        return (lax.rem(gx + side[0] + size_gx, size_gx), lax.rem(gy + side[1] + size_gy, size_gy))

    barrier = pltpu.get_barrier_semaphore()
    for side in reversed(SIDES):
        pl.semaphore_signal(barrier, inc=1, device_id=device(side), device_id_type=MESH)
    loads = [
        pltpu.make_async_copy(phase_in, h_buf.at[0], load_sem.at[0]),
        pltpu.make_async_copy(flow_in, f_buf.at[0], load_sem.at[1]),
        pltpu.make_async_copy(solid_in, solid, load_sem.at[2]),
    ]
    for load in loads:
        load.start()

    lanes = lax.broadcasted_iota(jnp.int32, (nz, ny), 1)
    first, last = lanes == 0, lanes == ny - 1

    def turn(tile, shift, axis):
        shift %= tile.shape[axis]
        return pltpu.roll(tile, shift, axis) if shift else tile

    def up(tile):
        return turn(tile, -1, 0)

    def down(tile):
        return turn(tile, 1, 0)

    def pushes(step):
        grouped = {}
        for x in range(nx):
            for n, (cx, cy, cz) in enumerate(PHASE_VELOCITIES):
                value = turn(h_buf[step, n, x], cz, 0)
                key = (cy, x + cx)
                grouped[key] = grouped[key] + value if key in grouped else value
        inside = {}
        for x in range(-1, nx + 1):
            inside[x] = (
                grouped[0, x]
                + jnp.where(first, 0.0, turn(grouped[1, x], 1, 1))
                + jnp.where(last, 0.0, turn(grouped[-1, x], -1, 1))
            )
        halves = {sign: jnp.zeros((half, ny), jnp.float32) for sign in (1, -1)}
        for key, slot in slots.items():
            if key[0] in ("h", "f"):
                kind, n, x = key
                velocities, buf = (PHASE_VELOCITIES, h_buf) if kind == "h" else (FLOW_VELOCITIES, f_buf)
                sign, tile = velocities[n][1], buf[step, n, x]
            else:
                sign = 1 if key[0][-1] == "+" else -1
                tile = inside[key[1]] if key[0][:4] == "edge" else grouped[sign, key[1]]
            source = ny - 1 if sign == 1 else 0
            for part in range(2):
                lane = slot + part * fold
                piece = turn(tile[part * half : (part + 1) * half], lane - source, 1)
                halves[sign] = jnp.where(lanes[:half] == lane, piece, halves[sign])
        packed = jnp.concatenate([halves[1], halves[-1]], axis=0)
        pack_out[step, 0] = inside[0]
        pack_out[step, 1] = packed
        pack_out[step, 2] = inside[nx - 1]
        return grouped, inside, packed

    def fill_slab(step):
        for place, sign in enumerate((-1, 1)):
            x = 0 if sign == -1 else nx - 1
            for k, (kind, n) in enumerate(CROSSING[sign]):
                slab_out[step, place, k] = (h_buf if kind == "h" else f_buf)[step, n, x]

    def slab_copies(step):
        return [
            pltpu.make_async_remote_copy(
                slab_out.at[step, place], slab_in.at[step, place],
                slab_send.at[step, place], slab_recv.at[step, place],
                device_id=device(SIDES[place]), device_id_type=MESH,
            )
            for place in range(2)
        ]

    def pack_copies(step):
        copies = []
        for place, side in enumerate(SIDES):
            begin, length = (0, 2) if place == 0 else (1, 2) if place == 1 else (1, 1)
            rows = pl.ds(0, nz) if side[1] == 0 else pl.ds(0 if side[1] == 1 else half, half)
            copies.append(
                pltpu.make_async_remote_copy(
                    pack_out.at[step, pl.ds(begin, length), rows],
                    pack_in.at[step, place, pl.ds(0, length), rows],
                    pack_send.at[step, place], pack_recv.at[step, place],
                    device_id=device(side), device_id_type=MESH,
                )
            )
        return copies

    tables = {"h": (PHASE_VELOCITIES, h_buf, h_moved), "f": (FLOW_VELOCITIES, f_buf, f_moved)}

    def origin(step, kind, n, x):
        velocities, buf, _ = tables[kind]
        source = x - velocities[n][0]
        side = -1 if source < 0 else 1 if source >= nx else 0
        if side == 0:
            return source, side, buf[step, n, source]
        return source, side, slab_in[step, 0 if side == 1 else 1, CROSSING[-side].index((kind, n))]

    def stage(step, from_slab):
        for kind, (velocities, _, moved) in tables.items():
            for n, (cx, cy, cz) in enumerate(velocities):
                for x in range(nx):
                    if (cy or cz) and (0 <= x - cx < nx) != from_slab:
                        tile = origin(step, kind, n, x)[2]
                        moved[n, x] = turn(turn(tile, cy, 1), cz, 0)

    def collide(step, own, store):
        grouped, inside, packed = own

        unfolded = {}

        def from_side(side, sign):
            if (side, sign) not in unfolded:
                begin = 0 if sign == 1 else half
                if side == (0, 0):
                    piece = packed[begin : begin + half]
                else:
                    place = SIDES.index((-side[0], -side[1]))
                    piece = pack_in[step, place, 1 if place == 0 else 0, begin : begin + half]
                unfolded[side, sign] = jnp.concatenate([piece, turn(piece, -fold, 1)], axis=0)
            return unfolded[side, sign]

        def pulled(kind, n, x):
            velocities, buf, moved = tables[kind]
            cx, cy, cz = velocities[n]
            source, side, tile = origin(step, kind, n, x)
            if cy or cz:
                tile = moved[n, x]
            if cy:
                column = turned_side((side, -cy), cz)
                slot = slots[kind, n, source - side * nx]
                edge = 0 if cy == 1 else ny - 1
                tile = jnp.where(lanes == edge, turn(column, edge - slot, 1), tile)
            return tile

        turned = {}

        def turned_side(side, cz):
            if (side, cz) not in turned:
                turned[side, cz] = turn(from_side(side, -side[1]), cz, 0)
            return turned[side, cz]

        phase_read = [[pulled("h", n, x) for n in range(15)] for x in range(nx)]
        flat_first = sorted(range(15), key=lambda n: abs(PHASE_VELOCITIES[n][1]))
        field = {x: functools.reduce(jnp.add, [phase_read[x][n] for n in flat_first]) for x in range(nx)}

        def column_sum(kind, x, gy_side):
            total = None
            for side in (0, 1, -1):
                at = x - side * nx
                if -1 <= at <= nx:
                    value = turn(from_side((side, gy_side), 1 if kind[-1] == "+" else -1), -slots[kind, at], 1)
                    total = value if total is None else total + value
            return total

        for x, edge_layer, side in ((-1, nx - 1, -1), (nx, 0, 1)):
            place = SIDES.index((-side, 0))
            value = inside[x] + pack_in[step, place, 0 if place == 0 else 1]
            for kind, gy_side, where in (("push+", -1, 0), ("push-", 1, ny - 1)):
                added = None
                for across in (0, side):
                    at = x - across * nx
                    term = turn(from_side((across, gy_side), -gy_side), where - slots[kind, at], 1)
                    added = term if added is None else added + term
                value = value + jnp.where(lanes == where, added, 0.0)
            field[x] = value

        flat, sideways, steep, deep = {}, {}, {}, {}
        star = {}
        for x in range(-1, nx + 1):
            phi = field[x]
            before = column_sum("push-", x, 0) + column_sum("edge+", x, -1)
            after = turn(column_sum("push+", x, 0) + column_sum("edge-", x, 1), ny - 1, 1)
            left = jnp.where(first, before, turn(phi, 1, 1))
            right = jnp.where(last, after, turn(phi, -1, 1))
            above, below = up(phi), down(phi)
            flat[x] = left + right
            sideways[x] = right - left
            steep[x] = above - below
            deep[x] = above + below
            star[x] = 2.0 * phi + flat[x] + deep[x]

        for x in range(nx):
            phi = field[x]
            dy, ys = sideways[x], flat[x]
            ys_up, ys_down = up(ys), down(ys)
            dx_grad = (star[x + 1] - star[x - 1]) * (1.0 / 12.0)
            dy_grad = (2.0 * dy + sideways[x + 1] + sideways[x - 1] + up(dy) + down(dy)) * (1.0 / 12.0)
            dz_grad = (2.0 * steep[x] + steep[x + 1] + steep[x - 1] + ys_up - ys_down) * (1.0 / 12.0)
            ringed = star[x + 1] + star[x - 1] + 2.0 * (ys + deep[x]) + ys_up + ys_down
            laplacian = ringed * (1.0 / 6.0) - 4.0 * phi
            gradient = (dx_grad, dy_grad, dz_grad)
            squared = dx_grad * dx_grad + dy_grad * dy_grad + dz_grad * dz_grad
            scaling = lax.rsqrt(jnp.maximum(squared, GRADIENT_FLOOR * GRADIENT_FLOOR))
            clipped = jnp.clip(phi, 0.0, 1.0)
            inv_density = 1.0 / (1.0 + 2.0 * clipped)
            inv_time = 1.0 / (0.6 + 0.4 * clipped)
            potential = 4.0 * BETA * phi * (phi - 1.0) * (phi - 0.5) - KAPPA * laplacian
            force = [potential * component for component in gradient]
            read = [pulled("f", n, x) for n in range(19)]
            pressure = functools.reduce(jnp.add, read)
            velocity = []
            for coordinate in range(3):
                moment = 0.5 * force[coordinate]
                for n in range(19):
                    if FLOW_VELOCITIES[n][coordinate] == 1:
                        moment = moment + read[n]
                    elif FLOW_VELOCITIES[n][coordinate] == -1:
                        moment = moment - read[n]
                velocity.append(moment * inv_density)
            speed_sq = velocity[0] * velocity[0] + velocity[1] * velocity[1] + velocity[2] * velocity[2]
            force_factor = 3.0 * (1.0 - 0.5 * inv_time) * inv_density
            keep = 1.0 - inv_time
            drift = [3.0 * inv_time * velocity[k] + force_factor * force[k] for k in range(3)]
            level = inv_time * (pressure - 1.5 * speed_sq)
            curve = 4.5 * inv_time
            solid_cells = solid[x] > 0

            def along(vector, values):
                total = None
                for c, value in zip(vector, values):
                    if c == 0:
                        continue
                    if total is None:
                        total = value
                        assert c == 1
                    else:
                        total = total + value if c == 1 else total - value
                return total

            store("f", 0, x, jnp.where(solid_cells, read[0], read[0] * keep + FLOW_WEIGHTS[0] * level))
            for weight in sorted(set(FLOW_WEIGHTS[1:])):
                level_w, curve_w = weight * level, weight * curve
                drift_w = [weight * value for value in drift]
                for n in range(1, 19):
                    vector = FLOW_VELOCITIES[n]
                    if FLOW_WEIGHTS[n] != weight or [c for c in vector if c][0] != 1:
                        continue
                    m = opposite(FLOW_VELOCITIES, n)
                    speed = along(vector, velocity)
                    even = level_w + curve_w * (speed * speed)
                    odd = along(vector, drift_w)
                    store("f", n, x, jnp.where(solid_cells, read[m], read[n] * keep + (even + odd)))
                    store("f", m, x, jnp.where(solid_cells, read[n], read[m] * keep + (even - odd)))

            gain = 1.0 / PHASE_RELAX
            interface = PHASE_LAMBDA * phi * (1.0 - phi) * scaling
            tilt = [3.0 * phi * velocity[k] + interface * gradient[k] for k in range(3)]
            pops = phase_read[x]
            store("h", 0, x, jnp.where(solid_cells, pops[0], (1.0 - gain) * pops[0] + gain * PHASE_WEIGHTS[0] * phi))
            for weight in sorted(set(PHASE_WEIGHTS[1:])):
                phi_w = (gain * weight) * phi
                tilt_w = [(gain * weight) * value for value in tilt]
                for n in range(1, 15):
                    vector = PHASE_VELOCITIES[n]
                    if PHASE_WEIGHTS[n] != weight or [c for c in vector if c][0] != 1:
                        continue
                    m = opposite(PHASE_VELOCITIES, n)
                    odd = along(vector, tilt_w)
                    store("h", n, x, jnp.where(solid_cells, pops[m], (1.0 - gain) * pops[n] + (phi_w + odd)))
                    store("h", m, x, jnp.where(solid_cells, pops[n], (1.0 - gain) * pops[m] + (phi_w - odd)))

    for load in loads:
        load.wait()
    for step in range(STEPS):
        own = pushes(step)
        if step == 0:
            fill_slab(step)
            pl.semaphore_wait(barrier, len(SIDES))
        packs = pack_copies(step)
        for copy in reversed(packs):
            copy.start()
        if step > 0:
            fill_slab(step)
        slabs = slab_copies(step)
        for copy in slabs:
            copy.start()
        stage(step, False)
        for copy in packs + slabs:
            copy.wait_send()
        for copy in slabs:
            copy.wait_recv()
        stage(step, True)
        for copy in packs:
            copy.wait_recv()

        def store(kind, n, x, value):
            if step + 1 == STEPS:
                (phase_out if kind == "h" else flow_out)[n, x] = value
            else:
                (h_buf if kind == "h" else f_buf)[step + 1, n, x] = value

        collide(step, own, store)


def write_back(phase, flow, phase_out, flow_out, sems):
    copies = [
        pltpu.make_async_copy(phase, phase_out, sems.at[0]),
        pltpu.make_async_copy(flow, flow_out, sems.at[1]),
    ]
    for copy in copies:
        copy.start()
    for copy in copies:
        copy.wait()


def shards(size_gx, size_gy, phase_pops, flow_pops, solid_flags):
    nx, nz, ny = solid_flags.shape
    f32 = jnp.float32
    crossing = len(CROSSING[1])
    anywhere = pl.BlockSpec(memory_space=pl.ANY)
    shapes = (phase_pops.shape, flow_pops.shape)
    on_chip = pl.BlockSpec(memory_space=pltpu.VMEM)
    results = pl.pallas_call(
        functools.partial(kernel, size_gx, size_gy),
        out_shape=tuple(pltpu.VMEM(shape, f32) for shape in shapes),
        in_specs=[anywhere] * 3,
        out_specs=(on_chip, on_chip),
        scratch_shapes=[
            pltpu.VMEM((STEPS,) + phase_pops.shape, f32),
            pltpu.VMEM((STEPS,) + flow_pops.shape, f32),
            pltpu.VMEM(phase_pops.shape, f32),
            pltpu.VMEM(flow_pops.shape, f32),
            pltpu.VMEM((nx, nz, ny), jnp.int32),
            pltpu.VMEM((STEPS, 2, crossing, nz, ny), f32),
            pltpu.VMEM((STEPS, 2, crossing, nz, ny), f32),
            pltpu.VMEM((STEPS, 3, nz, ny), f32),
            pltpu.VMEM((STEPS, len(SIDES), 2, nz, ny), f32),
            pltpu.SemaphoreType.DMA((3,)),
            pltpu.SemaphoreType.DMA((STEPS, 2)),
            pltpu.SemaphoreType.DMA((STEPS, 2)),
            pltpu.SemaphoreType.DMA((STEPS, len(SIDES))),
            pltpu.SemaphoreType.DMA((STEPS, len(SIDES))),
        ],
        compiler_params=pltpu.CompilerParams(collective_id=0, has_side_effects=True),
    )(phase_pops, flow_pops, solid_flags)
    return pl.pallas_call(
        write_back,
        out_shape=tuple(jax.ShapeDtypeStruct(shape, f32) for shape in shapes),
        in_specs=[on_chip, on_chip],
        out_specs=(anywhere, anywhere),
        scratch_shapes=[pltpu.SemaphoreType.DMA((2,))],
    )(*[pltpu.with_memory_space_constraint(r, pltpu.VMEM) for r in results])


def solution(mesh):
    placed = P(None, "gx", None, "gy")
    return jax.shard_map(
        functools.partial(shards, mesh.shape["gx"], mesh.shape["gy"]),
        mesh=mesh,
        in_specs=(placed, placed, P("gx", None, "gy")),
        out_specs=(placed, placed),
        check_vma=False,
    )
```

```python
import functools

import jax
import jax.numpy as jnp
from jax import lax
from jax.experimental import pallas as pl
from jax.experimental.pallas import tpu as pltpu
from jax.sharding import PartitionSpec as P

STEPS = 2
PHASE_VELOCITIES = [
    (0, 0, 0), (1, 0, 0), (-1, 0, 0), (0, 1, 0), (0, -1, 0), (0, 0, 1), (0, 0, -1),
    (1, 1, 1), (1, 1, -1), (1, -1, 1), (1, -1, -1),
    (-1, 1, 1), (-1, 1, -1), (-1, -1, 1), (-1, -1, -1),
]
PHASE_WEIGHTS = [2.0 / 9.0] + [1.0 / 9.0] * 6 + [1.0 / 72.0] * 8
FLOW_VELOCITIES = [
    (0, 0, 0), (1, 0, 0), (-1, 0, 0), (0, 1, 0), (0, -1, 0), (0, 0, 1), (0, 0, -1),
    (1, 1, 0), (1, -1, 0), (-1, 1, 0), (-1, -1, 0),
    (1, 0, 1), (1, 0, -1), (-1, 0, 1), (-1, 0, -1),
    (0, 1, 1), (0, 1, -1), (0, -1, 1), (0, -1, -1),
]
FLOW_WEIGHTS = [1.0 / 3.0] + [1.0 / 18.0] * 6 + [1.0 / 36.0] * 12
SURFACE_TENSION = 0.05
INTERFACE_WIDTH = 4.0
GRADIENT_FLOOR = 0.1
PHASE_LAMBDA = 0.3
PHASE_RELAX = 0.8
BETA = 12.0 * SURFACE_TENSION / INTERFACE_WIDTH
KAPPA = 1.5 * SURFACE_TENSION * INTERFACE_WIDTH

MESH = pl.DeviceIdType.MESH
SIDES = [(-1, 0), (1, 0), (0, -1), (0, 1), (-1, -1), (-1, 1), (1, -1), (1, 1)]


def moving(velocities, coordinate, sign):
    return [n for n, vector in enumerate(velocities) if vector[coordinate] == sign]


CROSSING = {
    sign: [("h", n) for n in moving(PHASE_VELOCITIES, 0, sign)]
    + [("f", n) for n in moving(FLOW_VELOCITIES, 0, sign)]
    for sign in (1, -1)
}


def opposite(velocities, n):
    vector = velocities[n]
    return velocities.index((-vector[0], -vector[1], -vector[2]))


def slot_table(nx):
    slots = {}
    for sign, mark in ((1, "+"), (-1, "-")):
        keys = []
        for kind, velocities in (("h", PHASE_VELOCITIES), ("f", FLOW_VELOCITIES)):
            keys += [(kind, n, x) for n in moving(velocities, 1, sign) for x in range(nx)]
        for kind in ("edge", "push"):
            keys += [(kind + mark, x) for x in range(-1, nx + 1)]
        slots.update({key: slot for slot, key in enumerate(keys)})
    return slots


def kernel(
    size_gx, size_gy, phase_in, flow_in, solid_in, phase_out, flow_out,
    h_buf, f_buf, h_moved, f_moved, solid, slab_out, slab_in, pack_out, pack_in,
    load_sem, slab_send, slab_recv, pack_send, pack_recv,
):
    nx, nz, ny = solid.shape
    slots = slot_table(nx)
    half, fold = nz // 2, ny // 2
    assert max(slots.values()) < fold
    gx, gy = lax.axis_index("gx"), lax.axis_index("gy")

    def device(side):
        return (lax.rem(gx + side[0] + size_gx, size_gx), lax.rem(gy + side[1] + size_gy, size_gy))

    barrier = pltpu.get_barrier_semaphore()
    for side in reversed(SIDES):
        pl.semaphore_signal(barrier, inc=1, device_id=device(side), device_id_type=MESH)
    loads = [
        pltpu.make_async_copy(phase_in, h_buf.at[0], load_sem.at[0]),
        pltpu.make_async_copy(flow_in, f_buf.at[0], load_sem.at[1]),
        pltpu.make_async_copy(solid_in, solid, load_sem.at[2]),
    ]
    for load in loads:
        load.start()

    lanes = lax.broadcasted_iota(jnp.int32, (nz, ny), 1)
    first, last = lanes == 0, lanes == ny - 1

    def turn(tile, shift, axis):
        shift %= tile.shape[axis]
        return pltpu.roll(tile, shift, axis) if shift else tile

    def up(tile):
        return turn(tile, -1, 0)

    def down(tile):
        return turn(tile, 1, 0)

    def pushes(step):
        grouped = {}
        for x in range(nx):
            for n, (cx, cy, cz) in enumerate(PHASE_VELOCITIES):
                value = turn(h_buf[step, n, x], cz, 0)
                key = (cy, x + cx)
                grouped[key] = grouped[key] + value if key in grouped else value
        inside = {}
        for x in range(-1, nx + 1):
            inside[x] = (
                grouped[0, x]
                + jnp.where(first, 0.0, turn(grouped[1, x], 1, 1))
                + jnp.where(last, 0.0, turn(grouped[-1, x], -1, 1))
            )
        halves = {sign: jnp.zeros((half, ny), jnp.float32) for sign in (1, -1)}
        for key, slot in slots.items():
            if key[0] in ("h", "f"):
                kind, n, x = key
                velocities, buf = (PHASE_VELOCITIES, h_buf) if kind == "h" else (FLOW_VELOCITIES, f_buf)
                sign, tile = velocities[n][1], buf[step, n, x]
            else:
                sign = 1 if key[0][-1] == "+" else -1
                tile = inside[key[1]] if key[0][:4] == "edge" else grouped[sign, key[1]]
            source = ny - 1 if sign == 1 else 0
            for part in range(2):
                lane = slot + part * fold
                piece = turn(tile[part * half : (part + 1) * half], lane - source, 1)
                halves[sign] = jnp.where(lanes[:half] == lane, piece, halves[sign])
        packed = jnp.concatenate([halves[1], halves[-1]], axis=0)
        pack_out[step, 0] = inside[0]
        pack_out[step, 1] = packed
        pack_out[step, 2] = inside[nx - 1]
        return grouped, inside, packed

    def fill_slab(step):
        for place, sign in enumerate((-1, 1)):
            x = 0 if sign == -1 else nx - 1
            for k, (kind, n) in enumerate(CROSSING[sign]):
                slab_out[step, place, k] = (h_buf if kind == "h" else f_buf)[step, n, x]

    def slab_copies(step):
        return [
            pltpu.make_async_remote_copy(
                slab_out.at[step, place], slab_in.at[step, place],
                slab_send.at[step, place], slab_recv.at[step, place],
                device_id=device(SIDES[place]), device_id_type=MESH,
            )
            for place in range(2)
        ]

    def pack_copies(step):
        copies = []
        for place, side in enumerate(SIDES):
            begin, length = (0, 2) if place == 0 else (1, 2) if place == 1 else (1, 1)
            rows = pl.ds(0, nz) if side[1] == 0 else pl.ds(0 if side[1] == 1 else half, half)
            copies.append(
                pltpu.make_async_remote_copy(
                    pack_out.at[step, pl.ds(begin, length), rows],
                    pack_in.at[step, place, pl.ds(0, length), rows],
                    pack_send.at[step, place], pack_recv.at[step, place],
                    device_id=device(side), device_id_type=MESH,
                )
            )
        return copies

    tables = {"h": (PHASE_VELOCITIES, h_buf, h_moved), "f": (FLOW_VELOCITIES, f_buf, f_moved)}

    def origin(step, kind, n, x):
        velocities, buf, _ = tables[kind]
        source = x - velocities[n][0]
        side = -1 if source < 0 else 1 if source >= nx else 0
        if side == 0:
            return source, side, buf[step, n, source]
        return source, side, slab_in[step, 0 if side == 1 else 1, CROSSING[-side].index((kind, n))]

    def stage(step, from_slab):
        for kind, (velocities, _, moved) in tables.items():
            for n, (cx, cy, cz) in enumerate(velocities):
                for x in range(nx):
                    if (cy or cz) and (0 <= x - cx < nx) != from_slab:
                        tile = origin(step, kind, n, x)[2]
                        moved[n, x] = turn(turn(tile, cy, 1), cz, 0)

    def collide(step, own, store):
        grouped, inside, packed = own

        unfolded = {}

        def from_side(side, sign):
            if (side, sign) not in unfolded:
                begin = 0 if sign == 1 else half
                if side == (0, 0):
                    piece = packed[begin : begin + half]
                else:
                    place = SIDES.index((-side[0], -side[1]))
                    piece = pack_in[step, place, 1 if place == 0 else 0, begin : begin + half]
                unfolded[side, sign] = jnp.concatenate([piece, turn(piece, -fold, 1)], axis=0)
            return unfolded[side, sign]

        def pulled(kind, n, x):
            velocities, buf, moved = tables[kind]
            cx, cy, cz = velocities[n]
            source, side, tile = origin(step, kind, n, x)
            if cy or cz:
                tile = moved[n, x]
            if cy:
                column = turned_side((side, -cy), cz)
                slot = slots[kind, n, source - side * nx]
                edge = 0 if cy == 1 else ny - 1
                tile = jnp.where(lanes == edge, turn(column, edge - slot, 1), tile)
            return tile

        turned = {}

        def turned_side(side, cz):
            if (side, cz) not in turned:
                turned[side, cz] = turn(from_side(side, -side[1]), cz, 0)
            return turned[side, cz]

        phase_read = [[pulled("h", n, x) for n in range(15)] for x in range(nx)]
        flat_first = sorted(range(15), key=lambda n: abs(PHASE_VELOCITIES[n][1]))
        field = {x: functools.reduce(jnp.add, [phase_read[x][n] for n in flat_first]) for x in range(nx)}

        reads = [[pulled("f", n, x) for n in range(19)] for x in range(nx)]

        def column_sum(kind, x, gy_side):
            total = None
            for side in (0, 1, -1):
                at = x - side * nx
                if -1 <= at <= nx:
                    value = turn(from_side((side, gy_side), 1 if kind[-1] == "+" else -1), -slots[kind, at], 1)
                    total = value if total is None else total + value
            return total

        for x, edge_layer, side in ((-1, nx - 1, -1), (nx, 0, 1)):
            place = SIDES.index((-side, 0))
            value = inside[x] + pack_in[step, place, 0 if place == 0 else 1]
            for kind, gy_side, where in (("push+", -1, 0), ("push-", 1, ny - 1)):
                added = None
                for across in (0, side):
                    at = x - across * nx
                    term = turn(from_side((across, gy_side), -gy_side), where - slots[kind, at], 1)
                    added = term if added is None else added + term
                value = value + jnp.where(lanes == where, added, 0.0)
            field[x] = value

        flat, sideways, steep, deep = {}, {}, {}, {}
        star = {}
        for x in range(-1, nx + 1):
            phi = field[x]
            before = column_sum("push-", x, 0) + column_sum("edge+", x, -1)
            after = turn(column_sum("push+", x, 0) + column_sum("edge-", x, 1), ny - 1, 1)
            left = jnp.where(first, before, turn(phi, 1, 1))
            right = jnp.where(last, after, turn(phi, -1, 1))
            above, below = up(phi), down(phi)
            flat[x] = left + right
            sideways[x] = right - left
            steep[x] = above - below
            deep[x] = above + below
            star[x] = 2.0 * phi + flat[x] + deep[x]

        for x in range(nx):
            phi = field[x]
            dy, ys = sideways[x], flat[x]
            ys_up, ys_down = up(ys), down(ys)
            dx_grad = (star[x + 1] - star[x - 1]) * (1.0 / 12.0)
            dy_grad = (2.0 * dy + sideways[x + 1] + sideways[x - 1] + up(dy) + down(dy)) * (1.0 / 12.0)
            dz_grad = (2.0 * steep[x] + steep[x + 1] + steep[x - 1] + ys_up - ys_down) * (1.0 / 12.0)
            ringed = star[x + 1] + star[x - 1] + 2.0 * (ys + deep[x]) + ys_up + ys_down
            laplacian = ringed * (1.0 / 6.0) - 4.0 * phi
            gradient = (dx_grad, dy_grad, dz_grad)
            squared = dx_grad * dx_grad + dy_grad * dy_grad + dz_grad * dz_grad
            scaling = lax.rsqrt(jnp.maximum(squared, GRADIENT_FLOOR * GRADIENT_FLOOR))
            clipped = jnp.clip(phi, 0.0, 1.0)
            inv_density = 1.0 / (1.0 + 2.0 * clipped)
            inv_time = 1.0 / (0.6 + 0.4 * clipped)
            potential = 4.0 * BETA * phi * (phi - 1.0) * (phi - 0.5) - KAPPA * laplacian
            force = [potential * component for component in gradient]
            read = reads[x]
            pressure = functools.reduce(jnp.add, read)
            velocity = []
            for coordinate in range(3):
                moment = 0.5 * force[coordinate]
                for n in range(19):
                    if FLOW_VELOCITIES[n][coordinate] == 1:
                        moment = moment + read[n]
                    elif FLOW_VELOCITIES[n][coordinate] == -1:
                        moment = moment - read[n]
                velocity.append(moment * inv_density)
            speed_sq = velocity[0] * velocity[0] + velocity[1] * velocity[1] + velocity[2] * velocity[2]
            force_factor = 3.0 * (1.0 - 0.5 * inv_time) * inv_density
            keep = 1.0 - inv_time
            drift = [3.0 * inv_time * velocity[k] + force_factor * force[k] for k in range(3)]
            level = inv_time * (pressure - 1.5 * speed_sq)
            curve = 4.5 * inv_time
            solid_cells = solid[x] > 0

            def along(vector, values):
                total = None
                for c, value in zip(vector, values):
                    if c == 0:
                        continue
                    if total is None:
                        total = value
                        assert c == 1
                    else:
                        total = total + value if c == 1 else total - value
                return total

            store("f", 0, x, jnp.where(solid_cells, read[0], read[0] * keep + FLOW_WEIGHTS[0] * level))
            for weight in sorted(set(FLOW_WEIGHTS[1:])):
                level_w, curve_w = weight * level, weight * curve
                drift_w = [weight * value for value in drift]
                for n in range(1, 19):
                    vector = FLOW_VELOCITIES[n]
                    if FLOW_WEIGHTS[n] != weight or [c for c in vector if c][0] != 1:
                        continue
                    m = opposite(FLOW_VELOCITIES, n)
                    speed = along(vector, velocity)
                    even = level_w + curve_w * (speed * speed)
                    odd = along(vector, drift_w)
                    store("f", n, x, jnp.where(solid_cells, read[m], read[n] * keep + (even + odd)))
                    store("f", m, x, jnp.where(solid_cells, read[n], read[m] * keep + (even - odd)))

            gain = 1.0 / PHASE_RELAX
            interface = PHASE_LAMBDA * phi * (1.0 - phi) * scaling
            tilt = [3.0 * phi * velocity[k] + interface * gradient[k] for k in range(3)]
            pops = phase_read[x]
            store("h", 0, x, jnp.where(solid_cells, pops[0], (1.0 - gain) * pops[0] + gain * PHASE_WEIGHTS[0] * phi))
            for weight in sorted(set(PHASE_WEIGHTS[1:])):
                phi_w = (gain * weight) * phi
                tilt_w = [(gain * weight) * value for value in tilt]
                for n in range(1, 15):
                    vector = PHASE_VELOCITIES[n]
                    if PHASE_WEIGHTS[n] != weight or [c for c in vector if c][0] != 1:
                        continue
                    m = opposite(PHASE_VELOCITIES, n)
                    odd = along(vector, tilt_w)
                    store("h", n, x, jnp.where(solid_cells, pops[m], (1.0 - gain) * pops[n] + (phi_w + odd)))
                    store("h", m, x, jnp.where(solid_cells, pops[n], (1.0 - gain) * pops[m] + (phi_w - odd)))

    for load in loads:
        load.wait()
    for step in range(STEPS):
        own = pushes(step)
        if step == 0:
            fill_slab(step)
            pl.semaphore_wait(barrier, len(SIDES))
        packs = pack_copies(step)
        for copy in reversed(packs):
            copy.start()
        if step > 0:
            fill_slab(step)
        slabs = slab_copies(step)
        for copy in slabs:
            copy.start()
        stage(step, False)
        for copy in packs + slabs:
            copy.wait_send()
        for copy in slabs:
            copy.wait_recv()
        stage(step, True)
        for copy in packs:
            copy.wait_recv()

        def store(kind, n, x, value):
            if step + 1 == STEPS:
                (phase_out if kind == "h" else flow_out)[n, x] = value
            else:
                (h_buf if kind == "h" else f_buf)[step + 1, n, x] = value

        collide(step, own, store)


def write_back(phase, flow, phase_out, flow_out, sems):
    copies = [
        pltpu.make_async_copy(phase, phase_out, sems.at[0]),
        pltpu.make_async_copy(flow, flow_out, sems.at[1]),
    ]
    for copy in copies:
        copy.start()
    for copy in copies:
        copy.wait()


def shards(size_gx, size_gy, phase_pops, flow_pops, solid_flags):
    nx, nz, ny = solid_flags.shape
    f32 = jnp.float32
    crossing = len(CROSSING[1])
    anywhere = pl.BlockSpec(memory_space=pl.ANY)
    shapes = (phase_pops.shape, flow_pops.shape)
    on_chip = pl.BlockSpec(memory_space=pltpu.VMEM)
    results = pl.pallas_call(
        functools.partial(kernel, size_gx, size_gy),
        out_shape=tuple(pltpu.VMEM(shape, f32) for shape in shapes),
        in_specs=[anywhere] * 3,
        out_specs=(on_chip, on_chip),
        scratch_shapes=[
            pltpu.VMEM((STEPS,) + phase_pops.shape, f32),
            pltpu.VMEM((STEPS,) + flow_pops.shape, f32),
            pltpu.VMEM(phase_pops.shape, f32),
            pltpu.VMEM(flow_pops.shape, f32),
            pltpu.VMEM((nx, nz, ny), jnp.int32),
            pltpu.VMEM((STEPS, 2, crossing, nz, ny), f32),
            pltpu.VMEM((STEPS, 2, crossing, nz, ny), f32),
            pltpu.VMEM((STEPS, 3, nz, ny), f32),
            pltpu.VMEM((STEPS, len(SIDES), 2, nz, ny), f32),
            pltpu.SemaphoreType.DMA((3,)),
            pltpu.SemaphoreType.DMA((STEPS, 2)),
            pltpu.SemaphoreType.DMA((STEPS, 2)),
            pltpu.SemaphoreType.DMA((STEPS, len(SIDES))),
            pltpu.SemaphoreType.DMA((STEPS, len(SIDES))),
        ],
        compiler_params=pltpu.CompilerParams(collective_id=0, has_side_effects=True),
    )(phase_pops, flow_pops, solid_flags)
    return pl.pallas_call(
        write_back,
        out_shape=tuple(jax.ShapeDtypeStruct(shape, f32) for shape in shapes),
        in_specs=[on_chip, on_chip],
        out_specs=(anywhere, anywhere),
        scratch_shapes=[pltpu.SemaphoreType.DMA((2,))],
    )(*[pltpu.with_memory_space_constraint(r, pltpu.VMEM) for r in results])


def solution(mesh):
    placed = P(None, "gx", None, "gy")
    return jax.shard_map(
        functools.partial(shards, mesh.shape["gx"], mesh.shape["gy"]),
        mesh=mesh,
        in_specs=(placed, placed, P("gx", None, "gy")),
        out_specs=(placed, placed),
        check_vma=False,
    )
```
